128 devices in a mesh: dp: 4 (over z), tensor: 32 (over x, y, core).
Axes of the slice: x: 4, y: 4, z: 4, core: 2. Of those that a mesh axis runs over, the one named last changes fastest.
Arguments:
- tokens: bfloat16 [256, 128, 1536], P(('dp', 'tensor')), may hold values from -60 to 60
- cached: bfloat16 [256, 512, 1536], P(('dp', 'tensor')), may hold values from -60 to 60
- norm_gains: float32 [2, 1536], replicated, may hold values from 0.5 to 1.5
- w_qkv: bfloat16 [1536, 3072], replicated, may hold values from -0.15625 to 0.15625
- w_out: bfloat16 [1536, 1536], replicated, may hold values from -0.15625 to 0.15625
- mlp_weights: bfloat16 [3, 1536, 4096], P(None, None, 'tensor'), may hold values from -0.15625 to 0.15625
- request_order: int32 [256], replicated, may hold values from 0 to 255, as said below
- new_lengths: int32 [256], replicated, may hold values from 1 to 128, 20480 in all
- cached_lengths: int32 [256], replicated, may hold values from 0 to 384
- decode_slots: int32 [256], replicated, may hold values from 0 to 255, as said below
Outputs:
- layer_out: bfloat16 [256, 128, 1536], P(('dp', 'tensor'))
- kv_decode: bfloat16 [256, 512, 1536], P('dp', 'tensor')
The draws below stay inside these ranges and needn't reach their ends.
Inputs may be any that keep to these rules, and one draw needn't show every extreme that they name: `request_order`: each value once; the device at index k of dp+tensor holds prefill slots k * 2 to (k + 1) * 2 - 1. `decode_slots`: each value once; the 64 requests held by the prefill slots of one index of dp take exactly 16 slots of every aligned block of 64 decode slots.
All inputs are finite; a program needn't handle non-finite values.
Results may differ from the reference program's by a relative error of at most 0.015.
Values may be sent and summed in bfloat16 or wider, within the bound.
A program may use at most 192 MiB of HBM per device.

```python
import math
import jax
import jax.numpy as jnp
import numpy as np
from jax import lax

D = 1536
HEADS = 16
KV_HEADS = 8
HEAD_DIM = 96
FF = 4096
NEW = 128
CTX = 512
KVW = 1536
REQS = 256
GROUP_REQS = 64
SHARE = 16
N_TENSOR = 32


def dealing(key):
    groups = REQS // GROUP_REQS
    ordering = jax.random.permutation(jax.random.fold_in(key, 11), REQS)
    mixing = jax.vmap(lambda subkey: jax.random.permutation(subkey, GROUP_REQS))(jax.random.split(jax.random.fold_in(key, 12), groups))
    within = jax.vmap(lambda subkey: jax.random.permutation(subkey, GROUP_REQS))(jax.random.split(jax.random.fold_in(key, 13), groups))
    target = mixing // SHARE
    placed = jnp.arange(groups)[:, None] * SHARE + mixing % SHARE
    slot_rows = target * GROUP_REQS + within[target, placed]
    slot_table = jnp.zeros((REQS,), jnp.int32).at[ordering].set(slot_rows.reshape(REQS).astype(jnp.int32))
    return (ordering.astype(jnp.int32), slot_table)


def draw_request_order(key, part):
    return dealing(key)[0]


def draw_decode_slots(key, part):
    return dealing(key)[1]


def draw_cached_lengths(key, part):
    drawn = jax.random.randint(jax.random.fold_in(key, 21), (REQS,), 0, CTX - NEW + 1)
    longest = jax.random.randint(jax.random.fold_in(key, 22), (), 0, REQS)
    shortest = (longest + 1 + jax.random.randint(jax.random.fold_in(key, 23), (), 0, REQS - 1)) % REQS
    return drawn.at[longest].set(CTX - NEW).at[shortest].set(0).astype(jnp.int32)


def draw_cached(key, part):
    normal_part = jax.random.normal(jax.random.fold_in(key, 31), (REQS, CTX, KVW), jnp.float32)
    return jnp.clip(normal_part, -6.0, 6.0).astype(jnp.bfloat16)


def draw_tokens(key, part):
    normal_part = jax.random.normal(jax.random.fold_in(key, 41), (REQS, NEW, D), jnp.float32)
    return jnp.clip(normal_part, -6.0, 6.0).astype(jnp.bfloat16)


def block_levels(own_key, dims, cuts, smallest, largest):
    def one(axis_at, parts):
        draws = jax.random.uniform(jax.random.fold_in(jax.random.fold_in(own_key, 6), axis_at), (parts,), jnp.float32, smallest / len(cuts), largest / len(cuts))
        return jnp.repeat(jnp.exp(draws), dims[axis_at] // parts).reshape((-1,) + (1,) * (len(dims) - axis_at - 1))

    factor_of = one(*cuts[0])
    for cut in cuts[1:]:
        factor_of = factor_of * one(*cut)
    return factor_of


def length_profile(number_of, total, reach, lean):
    loads = [(1 << 20) // math.isqrt(standing ** lean) + 1 for standing in range(2, number_of + 1)]
    surplus, holding = total - reach - (number_of - 1), [1] * (number_of - 1)
    while surplus > 0:
        candidates = [i for i in range(number_of - 1) if holding[i] < reach]
        mass, left = sum([loads[i] for i in candidates]), surplus
        for i in candidates:
            extra = min(reach - holding[i], max(1, left * loads[i] // mass), surplus)
            holding[i] = holding[i] + extra
            surplus = surplus - extra
    return np.array([reach] + holding)


def uneven(stream_key, amount, total, limit, skew):
    if amount == 2:
        one = jax.random.randint(stream_key, (), max(1, total - limit), min(limit, total - 1) + 1)
        return jnp.stack([one, total - one])
    lengths = jnp.asarray(length_profile(amount, total, limit, skew), jnp.int32)
    twos = (amount - 1) // 2
    source_of, receiver = lengths[1:1 + 2 * twos:2], lengths[2:2 + 2 * twos:2]
    room = jnp.minimum(source_of - 1, limit - receiver)
    moved = jax.random.randint(jax.random.fold_in(stream_key, 1), (twos,), 0, 1 << 20) % (room + 1)
    lengths = lengths.at[1:1 + 2 * twos:2].set(source_of - moved).at[2:2 + 2 * twos:2].set(receiver + moved)
    return lengths[jax.random.permutation(jax.random.fold_in(stream_key, 2), amount)]


def bell_draw(stream_key, extent, scale, bound, pieces=(), kind=jnp.bfloat16):
    loudness = block_levels(stream_key, extent, pieces, -0.22, 0.18) if pieces else 1.0
    array = jax.random.normal(stream_key, extent, jnp.float32) * scale * loudness
    return jnp.minimum(jnp.maximum(array, -bound), bound).astype(kind)


def setup_inputs(seed: int = 0) -> dict:
    key_list = jax.random.split(jax.random.key(seed), 11)
    return {
        "tokens": draw_tokens(jax.random.fold_in(key_list[10], 71), 0),
        "cached": draw_cached(jax.random.fold_in(key_list[10], 71), 0),
        "norm_gains": jnp.clip(1.0 + 0.1 * jax.random.normal(key_list[2], (2, D), jnp.float32), 0.5, 1.5),
        "w_qkv": bell_draw(key_list[3], (D, D + KVW), D ** -0.5, 0.15625),
        "w_out": bell_draw(key_list[4], (D, D), D ** -0.5, 0.15625),
        "mlp_weights": bell_draw(key_list[5], (3, D, FF), D ** -0.5, 0.15625, ((2, 32),)),
        "request_order": draw_request_order(jax.random.fold_in(key_list[10], 71), 0),
        "new_lengths": uneven(key_list[7], REQS, REQS * NEW * 5 // 8, NEW, 2).astype(jnp.int32),
        "cached_lengths": draw_cached_lengths(jax.random.fold_in(key_list[10], 71), 0),
        "decode_slots": draw_decode_slots(jax.random.fold_in(key_list[10], 71), 0),
    }


epsilon = 1e-05
rope_base = 100000.0

def norm_rows(values, gain):
    widened = values.astype(jnp.float32)
    factor = lax.rsqrt(lax.optimization_barrier(jnp.mean(widened * widened, axis=-1, keepdims=True)) + epsilon)
    return (widened * factor * gain).astype(jnp.bfloat16)

def rotate(values, positions):
    half_dim = values.shape[-1] // 2
    frequency = rope_base ** (-2.0 * jnp.arange(half_dim, dtype=jnp.float32) / values.shape[-1])
    angles = positions[:, None, None] * frequency
    cosine = jnp.cos(angles)
    sine_part = jnp.sin(angles)
    leading = values[..., :half_dim]
    trailing = values[..., half_dim:]
    return jnp.concatenate([leading * cosine - trailing * sine_part, trailing * cosine + leading * sine_part], axis=-1)

def place_context(fresh_rows, cached_rows, new_count, cached_count):
    offsets = jnp.arange(NEW, dtype=jnp.int32)
    kept = jnp.where((offsets < new_count)[:, None], fresh_rows, jnp.zeros_like(fresh_rows))
    canvas = jnp.zeros((CTX, fresh_rows.shape[1]), fresh_rows.dtype)
    placed = lax.dynamic_update_slice_in_dim(canvas, kept, cached_count.astype(jnp.int32), 0)
    spots = jnp.arange(CTX, dtype=jnp.int32)
    return jnp.where((spots < cached_count)[:, None], cached_rows, placed)

def attend(queries, context, cached_count):
    group_size = HEADS // KV_HEADS
    key_width = KV_HEADS * HEAD_DIM
    key_heads = context[:, :key_width].reshape(CTX, KV_HEADS, HEAD_DIM).astype(jnp.float32)
    value_heads = context[:, key_width:].reshape(CTX, KV_HEADS, HEAD_DIM).astype(jnp.float32)
    grouped = queries.reshape(NEW, KV_HEADS, group_size, HEAD_DIM).astype(jnp.float32)
    scores = jnp.einsum('qkgd,pkd->kgqp', grouped, key_heads) * HEAD_DIM ** (-0.5)
    last_key = cached_count + jnp.arange(NEW, dtype=jnp.int32)
    allowed = jnp.arange(CTX, dtype=jnp.int32)[None, :] <= last_key[:, None]
    scores = jnp.where(allowed, scores, -jnp.inf)
    highest = lax.optimization_barrier(jnp.max(scores, axis=-1, keepdims=True))
    exponent = jnp.exp(scores - highest)
    weights = (exponent / lax.optimization_barrier(jnp.sum(exponent, axis=-1, keepdims=True))).astype(jnp.bfloat16)
    attended = jnp.einsum('kgqp,pkd->qkgd', weights.astype(jnp.float32), value_heads)
    return attended.reshape(NEW, HEADS * HEAD_DIM).astype(jnp.bfloat16)

def reference(tokens, cached, norm_gains, w_qkv, w_out, mlp_weights, request_order, new_lengths, cached_lengths, decode_slots):
    new_counts = new_lengths[request_order]
    cached_counts = cached_lengths[request_order]
    key_width = KV_HEADS * HEAD_DIM
    down_wide = mlp_weights[2].reshape(D, N_TENSOR, FF // N_TENSOR).astype(jnp.float32)

    def one_request(inputs):
        request_tokens, request_cache, new_count, cached_count = inputs
        normed = norm_rows(request_tokens, norm_gains[0])
        projected = jnp.dot(normed, w_qkv, preferred_element_type=jnp.float32)
        positions = (cached_count + jnp.arange(NEW, dtype=jnp.int32)).astype(jnp.float32)
        queries = rotate(projected[:, :D].reshape(NEW, HEADS, HEAD_DIM), positions).astype(jnp.bfloat16)
        key_rows = rotate(projected[:, D:D + key_width].reshape(NEW, KV_HEADS, HEAD_DIM), positions).reshape(NEW, key_width)
        fresh_rows = jnp.concatenate([key_rows, projected[:, D + key_width:]], axis=1).astype(jnp.bfloat16)
        context = place_context(fresh_rows, request_cache, new_count, cached_count)
        attended = attend(queries, context, cached_count)
        residual = (request_tokens.astype(jnp.float32) + jnp.dot(attended, w_out, preferred_element_type=jnp.float32)).astype(jnp.bfloat16)
        post_norm = norm_rows(residual, norm_gains[1])
        gate_out = jnp.dot(post_norm, mlp_weights[0], preferred_element_type=jnp.float32)
        up_out = jnp.dot(post_norm, mlp_weights[1], preferred_element_type=jnp.float32)
        activated = (jax.nn.silu(gate_out) * up_out).astype(jnp.bfloat16)
        spread = activated.reshape(NEW, N_TENSOR, FF // N_TENSOR).astype(jnp.float32)
        partial_sums = jnp.einsum('rmw,dmw->mrd', spread, down_wide).astype(jnp.bfloat16)
        mlp_sum = lax.optimization_barrier(jnp.sum(partial_sums.astype(jnp.float32), axis=0))
        live = (jnp.arange(NEW, dtype=jnp.int32) < new_count)[:, None]
        layer_rows = jnp.where(live, residual.astype(jnp.float32) + mlp_sum, 0.0).astype(jnp.bfloat16)
        return (layer_rows, context)
    outputs, contexts = lax.map(one_request, (tokens, cached, new_counts, cached_counts))
    request_at_slot = jnp.argsort(decode_slots)
    prefill_of_request = jnp.argsort(request_order)
    kv_decode = contexts[prefill_of_request[request_at_slot]]
    return (outputs, kv_decode)
```

```python
import functools

import jax
import jax.numpy as jnp
import numpy as np
from jax import lax
from jax.experimental import pallas as pl
from jax.experimental.pallas import tpu as pltpu
from jax.sharding import PartitionSpec as P

D = 1536
HEADS = 16
KV_HEADS = 8
HEAD_DIM = 96
NEW = 128
CTX = 512
KEYS = KV_HEADS * HEAD_DIM
RING = 4
CHIPS = RING * RING
MESH = pl.DeviceIdType.MESH

epsilon = 1e-05
rope_base = 100000.0
LANES = 384
TILE = 256
TILES = D // TILE


def messages():
    found = []

    def along(axis, shards, first):
        step = (1, 0) if axis == 0 else (0, 1)
        for shard in shards:
            for sign in (1, -1):
                found.append((shard, first, 2, (sign * step[0], sign * step[1]), "send"))
            for sign in (1, -1):
                source = (shard[0] - sign * step[0], shard[1] - sign * step[1])
                piece = first if sign == 1 else first + 1
                found.append((source, piece, 1, (sign * step[0], sign * step[1]), "pass"))

    along(0, [(0, 0)], 0)
    along(1, [(0, 0)], 2)
    along(1, [(0, 0)], 0)
    along(0, [(0, 0)], 2)
    along(1, [(-1, 0), (1, 0)], 0)
    along(0, [(0, -1), (0, 1)], 2)
    along(1, [(2, 0)], 0)
    along(0, [(0, 2)], 2)
    return found


MESSAGES = messages()
N_MSG = len(MESSAGES)


def wrapped(offset):
    return (offset[0] % RING, offset[1] % RING)


def arrival(message):
    shard, first, count, direction, _ = message
    return wrapped((shard[0] - direction[0], shard[1] - direction[1])), first, count


def stage_of(index):
    shard, first, count, _, _ = MESSAGES[index]
    if wrapped(shard) == (0, 0):
        return 0
    return 1 + max(stage_of(other) for other in sources(index))


def sources(index):
    shard, first, count, _, _ = MESSAGES[index]
    found = []
    for piece in range(first, first + count):
        for other, message in enumerate(MESSAGES):
            came, start, number = arrival(message)
            if came == wrapped(shard) and start <= piece < start + number:
                found.append(other)
    return sorted(set(found))


def norm_rows(values, gain):
    widened = values.astype(jnp.float32)
    factor = lax.rsqrt(jnp.mean(widened * widened, axis=-1, keepdims=True) + epsilon)
    return (widened * factor * gain).astype(jnp.bfloat16)


def dot(a, b):
    return lax.dot_general(a, b, (((1,), (0,)), ((), ())), preferred_element_type=jnp.float32)


def dot_nt(a, b):
    return lax.dot_general(a, b, (((1,), (1,)), ((), ())), preferred_element_type=jnp.float32)


def layer_kernel(
    index_ref,
    tokens_hbm,
    cached_hbm,
    gains_ref,
    turn_ref,
    rope_ref,
    w_qkv_hbm,
    w_out_hbm,
    own_hbm,
    layer_hbm,
    arrived_hbm,
    tokens,
    normed,
    w_qkv,
    w_out,
    context,
    weights,
    queries,
    fresh,
    attended,
    residual,
    posts,
    received_keys,
    received_values,
    arranged,
    activated,
    kept,
    own_sum,
    to_partner,
    from_partner,
    to_pair,
    from_pair,
    local_sem,
    weight_send,
    weight_recv,
    kv_send,
    kv_recv,
    deal_send,
    deal_recv,
    post_send,
    post_recv,
    part_send,
    part_recv,
):
    z = lax.axis_index("dp")
    t = lax.axis_index("tensor")
    x, y, core = t // 8, lax.rem(t // 2, RING), lax.rem(t, 2)
    half = lax.rem(z, 2)
    pair_z = z + 1 - 2 * half
    partner = t + 1 - 2 * core
    member = half * 2 + core

    def tensor_at(dx, dy, other=0):
        there = lax.rem(core + other, 2)
        return (lax.rem(x + dx + RING, RING) * RING + lax.rem(y + dy + RING, RING)) * 2 + there

    def shard_at(offset):
        return lax.rem(x + offset[0] + RING, RING) * RING + lax.rem(y + offset[1] + RING, RING)

    loads = [
        pltpu.make_async_copy(
            own_hbm.at[:, pl.ds(half * 64, 64), :],
            weights.at[:, pl.ds(shard_at((0, 0)) * 64, 64), :],
            local_sem.at[0],
        ),
        pltpu.make_async_copy(tokens_hbm, tokens, local_sem.at[1]),
        pltpu.make_async_copy(w_qkv_hbm, w_qkv, local_sem.at[2]),
        pltpu.make_async_copy(cached_hbm, context, local_sem.at[3]),
        pltpu.make_async_copy(w_out_hbm, w_out, local_sem.at[4]),
    ]
    for load in loads:
        load.start()

    barrier = pltpu.get_barrier_semaphore()

    @pl.loop(1, 32)
    def _(step):
        pl.semaphore_signal(
            barrier, inc=1, device_id=(z, lax.rem(t + step, 32)), device_id_type=MESH
        )

    @pl.loop(1, 4)
    def _(step):
        pl.semaphore_signal(
            barrier, inc=1, device_id=(lax.rem(z + step, 4), t), device_id_type=MESH
        )

    pl.semaphore_wait(barrier, 34)

    def weight_copy(index):
        shard, first, count, direction, _ = MESSAGES[index]
        rows = pl.ds(pl.multiple_of(shard_at(wrapped(shard)) * 64 + 16 * first, 16), 16 * count)
        return pltpu.make_async_remote_copy(
            src_ref=weights.at[:, rows, :],
            dst_ref=weights.at[:, rows, :],
            send_sem=weight_send.at[index],
            recv_sem=weight_recv.at[index],
            device_id=(z, tensor_at(*direction)),
            device_id_type=MESH,
        )

    def weight_arrival(index):
        shard, first, count = arrival(MESSAGES[index])
        rows = pl.ds(pl.multiple_of(shard_at(shard) * 64 + 16 * first, 16), 16 * count)
        pltpu.make_async_remote_copy(
            src_ref=weights.at[:, rows, :],
            dst_ref=weights.at[:, rows, :],
            send_sem=weight_send.at[index],
            recv_sem=weight_recv.at[index],
            device_id=(z, partner),
            device_id_type=MESH,
        ).wait_recv()

    heard = set()

    def weight_stage(number):
        for index in range(N_MSG):
            if stage_of(index) == number:
                for other in sources(index) if number else []:
                    if other not in heard:
                        heard.add(other)
                        weight_arrival(other)
                weight_copy(index).start()

    def weight_rest():
        for index in range(N_MSG):
            if index not in heard:
                weight_arrival(index)
        for index in range(N_MSG):
            weight_copy(index).wait_send()

    loads[0].wait()
    weight_stage(0)

    loads[1].wait()
    for j in range(2):
        normed[pl.ds(j * NEW, NEW), :] = norm_rows(tokens[j], gains_ref[0:1, :])
    loads[2].wait()

    lane = lax.broadcasted_iota(jnp.int32, (NEW, LANES), 1)
    leading = lax.rem(lane, HEAD_DIM) < HEAD_DIM // 2

    def rotated(values, j):
        cosine = turn_ref[j, 0:1, :] * rope_ref[0] - turn_ref[j, 1:2, :] * rope_ref[1]
        sine = turn_ref[j, 2:3, :] * rope_ref[0] + turn_ref[j, 3:4, :] * rope_ref[1]
        parts = []
        for n in range(values.shape[1] // LANES):
            part = values[:, n * LANES : (n + 1) * LANES]
            swapped = jnp.where(
                leading,
                pltpu.roll(part, LANES - HEAD_DIM // 2, 1),
                pltpu.roll(part, HEAD_DIM // 2, 1),
            )
            parts.append((part * cosine + swapped * sine).astype(jnp.bfloat16))
        return jnp.concatenate(parts, axis=1)

    def project(first):
        return dot(normed[...], w_qkv[:, first : first + KEYS])

    keys = project(D)
    for j in range(2):
        fresh[j, :, 0:KEYS] = rotated(keys[j * NEW : (j + 1) * NEW], j)
    values = project(D + KEYS)
    for j in range(2):
        fresh[j, :, KEYS:] = values[j * NEW : (j + 1) * NEW].astype(jnp.bfloat16)

    loads[3].wait()

    @pl.loop(0, 8)
    def _(step):
        j, block = step // 4, lax.rem(step, 4)
        new_count, cached_count = index_ref[64 + j], index_ref[66 + j]
        spot = block * 128 + lax.broadcasted_iota(jnp.int32, (128, NEW), 0)
        order = lax.broadcasted_iota(jnp.int32, (128, NEW), 1)
        chosen = (spot - cached_count == order) & (order < new_count)
        placed = dot(chosen.astype(jnp.bfloat16), fresh[j]).astype(jnp.bfloat16)
        rows = pl.ds(pl.multiple_of(block * 128, 128), 128)
        row = block * 128 + lax.broadcasted_iota(jnp.int32, (128, D), 0)
        context[j, rows, :] = jnp.where(row < cached_count, context[j, rows, :], placed)

    received = (received_keys, received_values)

    def kv_copy(part, step):
        dx, dy, dc = step // 8, lax.rem(step // 2, RING), lax.rem(step, 2)
        target = tensor_at(dx, dy, dc)
        columns = pl.ds(part * KEYS, KEYS)
        return pltpu.make_async_remote_copy(
            src_ref=context.at[:, pl.ds(pl.multiple_of(target * 16, 16), 16), columns],
            dst_ref=received[part].at[t],
            send_sem=kv_send.at[part, step],
            recv_sem=kv_recv.at[part, step],
            device_id=(z, target),
            device_id_type=MESH,
        )

    for part in range(2):

        @pl.loop(1, 32)
        def _(step):
            kv_copy(part, step).start()

    for part in range(2):
        for j in range(2):
            received[part][t, j] = context[
                j, pl.ds(pl.multiple_of(t * 16, 16), 16), part * KEYS : (part + 1) * KEYS
            ]

    for n in range(2):
        some = project(n * KEYS)
        for j in range(2):
            queries[j, :, n * KEYS : (n + 1) * KEYS] = rotated(some[j * NEW : (j + 1) * NEW], j)

    weight_stage(1)

    def attend(j):
        cached_count = index_ref[66 + j]
        spot = lax.broadcasted_iota(jnp.int32, (2 * NEW, CTX), 1)
        order = lax.rem(lax.broadcasted_iota(jnp.int32, (2 * NEW, CTX), 0), NEW)
        allowed = spot <= cached_count + order
        for h in range(KV_HEADS):
            at = h * 2 * HEAD_DIM
            both = jnp.concatenate(
                [queries[j, :, at : at + HEAD_DIM], queries[j, :, at + HEAD_DIM : at + 2 * HEAD_DIM]],
                axis=0,
            )
            key = context[j, :, h * HEAD_DIM : (h + 1) * HEAD_DIM]
            value = context[j, :, KEYS + h * HEAD_DIM : KEYS + (h + 1) * HEAD_DIM]
            scores = dot_nt(both, key) * HEAD_DIM ** (-0.5)
            scores = jnp.where(allowed, scores, -jnp.inf)
            exponent = jnp.exp(scores - jnp.max(scores, axis=-1, keepdims=True))
            total = jnp.sum(exponent, axis=-1, keepdims=True)
            mixed = (dot(exponent.astype(jnp.bfloat16), value) / total).astype(jnp.bfloat16)
            attended[j, :, at : at + 2 * HEAD_DIM] = jnp.concatenate(
                [mixed[:NEW], mixed[NEW:]], axis=1
            )

    def post_copy(kind, j):
        whose = member if kind < 2 else (1 - half) * 2 + core
        rows = posts.at[whose, pl.ds(j * NEW, NEW), :]
        return pltpu.make_async_remote_copy(
            src_ref=rows,
            dst_ref=rows,
            send_sem=post_send.at[kind, j],
            recv_sem=post_recv.at[kind, j],
            device_id=(pair_z, t) if kind == 1 else (z, partner),
            device_id_type=MESH,
        )

    def post_arrival(kind, j):
        whose = (half * 2 + 1 - core, (1 - half) * 2 + core, (1 - half) * 2 + 1 - core)[kind]
        rows = posts.at[whose, pl.ds(j * NEW, NEW), :]
        pltpu.make_async_remote_copy(
            src_ref=rows,
            dst_ref=rows,
            send_sem=post_send.at[kind, j],
            recv_sem=post_recv.at[kind, j],
            device_id=(z, partner),
            device_id_type=MESH,
        ).wait_recv()

    for j in range(2):
        attend(j)
        if j == 0:
            loads[4].wait()
        mixed = dot(attended[j], w_out[...])
        rounded = (tokens[j].astype(jnp.float32) + mixed).astype(jnp.bfloat16)
        residual[j] = rounded
        posts[member, pl.ds(j * NEW, NEW), :] = norm_rows(rounded, gains_ref[1:2, :])
        post_copy(1, j).start()
        post_copy(0, j).start()
        if j == 0:
            weight_stage(2)

    weight_stage(3)

    def deal_copy(part, step):
        target = lax.rem(z + step, 4)
        return pltpu.make_async_remote_copy(
            src_ref=arranged.at[part, pl.ds(pl.multiple_of(target * 16, 16), 16)],
            dst_ref=arrived_hbm.at[part, z],
            send_sem=deal_send.at[part, step],
            recv_sem=deal_recv.at[part, step],
            device_id=(target, t),
            device_id_type=MESH,
        )

    def own_deal(part):
        return pltpu.make_async_copy(
            arranged.at[part, pl.ds(pl.multiple_of(z * 16, 16), 16)],
            arrived_hbm.at[part, z],
            deal_send.at[part, 0],
        )

    def deal(part):
        @pl.loop(1, 32)
        def _(step):
            dx, dy, dc = step // 8, lax.rem(step // 2, RING), lax.rem(step, 2)
            source = (
                lax.rem(x - dx + RING, RING) * RING + lax.rem(y - dy + RING, RING)
            ) * 2 + lax.rem(core + dc, 2)
            pltpu.make_async_remote_copy(
                src_ref=received[part].at[source],
                dst_ref=received[part].at[source],
                send_sem=kv_send.at[part, step],
                recv_sem=kv_recv.at[part, step],
                device_id=(z, partner),
                device_id_type=MESH,
            ).wait_recv()

        @pl.loop(0, 64)
        def _(row):
            slot = index_ref[row]
            arranged[part, row] = received[part][slot // 2, lax.rem(slot, 2)]

        for step in range(1, 4):
            deal_copy(part, step).start()
        own_deal(part).start()

    for j in range(2):
        post_arrival(1, j)
        post_copy(2, j).start()

    deal(0)
    deal(1)

    for j in range(2):
        post_arrival(0, j)
        post_arrival(2, j)
    weight_rest()

    def hidden(which):
        @pl.loop(0, 4)
        def _(step):
            units = pl.ds(pl.multiple_of(step * TILE, TILE), TILE)
            for m in range(2):
                rows = posts[which * 2 + m]
                gate = dot_nt(rows, weights[0, units, :])
                up = dot_nt(rows, weights[1, units, :])
                activated[m, :, units] = (gate / (1.0 + jnp.exp(-gate)) * up).astype(jnp.bfloat16)

    def part_copy(kind, n):
        here, there = ((to_partner.at[0, n], from_partner.at[0, n]), (to_pair.at[n], from_pair.at[n]), (to_partner.at[1, n], from_partner.at[1, n]))[kind]
        return pltpu.make_async_remote_copy(
            src_ref=here,
            dst_ref=there,
            send_sem=part_send.at[kind, n],
            recv_sem=part_recv.at[kind, n],
            device_id=(pair_z, t) if kind == 1 else (z, partner),
            device_id_type=MESH,
        )

    def down(m, n):
        columns = pl.ds(pl.multiple_of(n * TILE, TILE), TILE)
        return dot(activated[m], weights[2, :, columns])

    def add_up(n):
        part_copy(0, n).wait_recv()
        to_pair[n] = (kept[n] + from_partner[0, n].astype(jnp.float32)).astype(jnp.bfloat16)
        part_copy(1, n).start()

    hidden(1 - half)

    @pl.loop(0, TILES)
    def _(n):
        to_partner[0, n] = down(1 - core, n).astype(jnp.bfloat16)
        part_copy(0, n).start()
        kept[n] = down(core, n)

        @pl.when(n > 0)
        def _():
            add_up(n - 1)

    add_up(TILES - 1)

    hidden(half)

    @pl.loop(0, TILES)
    def _(n):
        to_partner[1, n] = down(1 - core, n).astype(jnp.bfloat16)
        part_copy(2, n).start()
        own_sum[n] = down(core, n)

    for n in range(TILES):
        part_copy(2, n).wait_recv()
        part_copy(1, n).wait_recv()
        columns = slice(n * TILE, (n + 1) * TILE)
        for j in range(2):
            rows = slice(j * NEW, (j + 1) * NEW)
            row = lax.broadcasted_iota(jnp.int32, (NEW, TILE), 0)
            total = (
                residual[j, :, columns].astype(jnp.float32)
                + own_sum[n, rows]
                + from_partner[1, n, rows].astype(jnp.float32)
                + from_pair[n, rows].astype(jnp.float32)
            )
            tokens[j, :, columns] = jnp.where(row < index_ref[64 + j], total, 0.0).astype(jnp.bfloat16)
    store = pltpu.make_async_copy(tokens, layer_hbm, local_sem.at[1])
    store.start()

    for part in range(2):
        for step in range(1, 4):
            source = lax.rem(z - step + 4, 4)
            pltpu.make_async_remote_copy(
                src_ref=arranged.at[part, pl.ds(0, 16)],
                dst_ref=arrived_hbm.at[part, source],
                send_sem=deal_send.at[part, step],
                recv_sem=deal_recv.at[part, step],
                device_id=(source, t),
                device_id_type=MESH,
            ).wait_recv()
            deal_copy(part, step).wait_send()
        own_deal(part).wait()

        @pl.loop(1, 32)
        def _(step):
            kv_copy(part, step).wait_send()

    for kind in range(3):
        for j in range(2):
            post_copy(kind, j).wait_send()
        for n in range(TILES):
            part_copy(kind, n).wait_send()
    store.wait()


def gather_kernel(index_ref, arrived_hbm, out_hbm, rows, load_sem, store_sem):
    def load(s, part):
        source = index_ref[s]
        return pltpu.make_async_copy(
            arrived_hbm.at[part, source // 16, lax.rem(source, 16)],
            rows.at[s, :, pl.ds(part * KEYS, KEYS)],
            load_sem.at[s // 16],
        )

    def store(block):
        span = pl.ds(pl.multiple_of(block * 16, 16), 16)
        return pltpu.make_async_copy(rows.at[span], out_hbm.at[span], store_sem.at[block])

    @pl.loop(0, 64)
    def _(s):
        load(s, 0).start()
        load(s, 1).start()

    @pl.loop(0, 4)
    def _(block):
        span = pl.ds(pl.multiple_of(block * 16, 16), 16)
        pltpu.make_async_copy(rows.at[span], rows.at[span], load_sem.at[block]).wait()
        store(block).start()

    @pl.loop(0, 4)
    def _(block):
        store(block).wait()


def lookup(source_table, wanted):
    every_index = jnp.arange(source_table.shape[0], dtype=jnp.int32)
    matches = wanted[:, None] == every_index[None, :]
    return jnp.sum(jnp.where(matches, source_table[None, :], 0), axis=1)


def locate(source_table, wanted):
    every_index = jnp.arange(source_table.shape[0], dtype=jnp.int32)
    matches = source_table[None, :] == wanted[:, None]
    return jnp.sum(jnp.where(matches, every_index[None, :], 0), axis=1)


def frequencies():
    lane = np.arange(LANES) % HEAD_DIM
    return rope_base ** (-2.0 * (lane % (HEAD_DIM // 2)) / HEAD_DIM), np.where(lane < HEAD_DIM // 2, -1.0, 1.0)


def local(
    tokens,
    cached,
    norm_gains,
    w_qkv,
    w_out,
    mlp_weights,
    request_order,
    new_lengths,
    cached_lengths,
    decode_slots,
):
    group_reqs = 64
    local_reqs = 2
    group_index = lax.axis_index("dp")
    device_index = group_index * 32 + lax.axis_index("tensor")
    local_order = lax.dynamic_slice_in_dim(request_order, device_index * local_reqs, local_reqs)
    new_counts = lookup(new_lengths, local_order)
    cached_counts = lookup(cached_lengths, local_order)

    group_order = lax.dynamic_slice_in_dim(request_order, group_index * group_reqs, group_reqs)
    row_slots = lookup(decode_slots, group_order)
    ordinal = jnp.arange(group_reqs, dtype=jnp.int32)
    rank = jnp.sum((row_slots[None, :] < row_slots[:, None]).astype(jnp.int32), axis=1)
    by_slot = jnp.sum(jnp.where(rank[None, :] == ordinal[:, None], ordinal[None, :], 0), axis=1)
    slot_ids = group_index * group_reqs + ordinal
    owners = locate(request_order, locate(decode_slots, slot_ids)) // group_reqs
    same_owner = (owners[:, None] == owners[None, :]) & (ordinal[None, :] < ordinal[:, None])
    source_rows = owners * 16 + jnp.sum(same_owner.astype(jnp.int32), axis=1)

    frequency, sign = frequencies()
    angle = np.arange(NEW)[:, None] * frequency[None, :]
    rope = jnp.asarray(np.stack([np.cos(angle), np.sin(angle)]), jnp.float32)
    turn = cached_counts.astype(jnp.float32)[:, None] * jnp.asarray(frequency, jnp.float32)[None, :]
    cosine, sine = jnp.cos(turn), jnp.sin(turn)
    signs = jnp.asarray(sign, jnp.float32)[None, :]
    turns = jnp.stack([cosine, sine, sine * signs, cosine * signs], axis=1)

    index = jnp.concatenate([by_slot, new_counts, cached_counts])
    own = jnp.transpose(mlp_weights, (0, 2, 1))

    bf16 = jnp.bfloat16
    smem = pl.BlockSpec(memory_space=pltpu.SMEM)
    vmem = pl.BlockSpec(memory_space=pltpu.VMEM)
    anywhere = pl.BlockSpec(memory_space=pl.ANY)
    dma = pltpu.SemaphoreType.DMA
    layer_out, arrived = pl.pallas_call(
        layer_kernel,
        out_shape=(
            jax.ShapeDtypeStruct((2, NEW, D), bf16),
            jax.ShapeDtypeStruct((2, 4, 16, 16, KEYS), bf16),
        ),
        in_specs=[smem, anywhere, anywhere, vmem, vmem, vmem, anywhere, anywhere, anywhere],
        out_specs=(anywhere, anywhere),
        scratch_shapes=[
            pltpu.VMEM((2, NEW, D), bf16),
            pltpu.VMEM((2 * NEW, D), bf16),
            pltpu.VMEM((D, 2 * D), bf16),
            pltpu.VMEM((D, D), bf16),
            pltpu.VMEM((2, CTX, D), bf16),
            pltpu.VMEM((3, 1024, D), bf16),
            pltpu.VMEM((2, NEW, D), bf16),
            pltpu.VMEM((2, NEW, D), bf16),
            pltpu.VMEM((2, NEW, D), bf16),
            pltpu.VMEM((2, NEW, D), bf16),
            pltpu.VMEM((4, 2 * NEW, D), bf16),
            pltpu.VMEM((32, 2, 16, KEYS), bf16),
            pltpu.VMEM((32, 2, 16, KEYS), bf16),
            pltpu.VMEM((2, 64, 16, KEYS), bf16),
            pltpu.VMEM((2, 2 * NEW, 1024), bf16),
            pltpu.VMEM((TILES, 2 * NEW, TILE), jnp.float32),
            pltpu.VMEM((TILES, 2 * NEW, TILE), jnp.float32),
            pltpu.VMEM((2, TILES, 2 * NEW, TILE), bf16),
            pltpu.VMEM((2, TILES, 2 * NEW, TILE), bf16),
            pltpu.VMEM((TILES, 2 * NEW, TILE), bf16),
            pltpu.VMEM((TILES, 2 * NEW, TILE), bf16),
            dma((5,)),
            dma((N_MSG,)),
            dma((N_MSG,)),
            dma((2, 32)),
            dma((2, 32)),
            dma((2, 4)),
            dma((2, 4)),
            dma((3, 2)),
            dma((3, 2)),
            dma((3, TILES)),
            dma((3, TILES)),
        ],
        compiler_params=pltpu.CompilerParams(
            collective_id=0, has_side_effects=True, vmem_limit_bytes=67_000_000
        ),
        name="layer",
    )(index, tokens, cached, norm_gains, turns, rope, w_qkv, w_out, own)

    kv_decode = pl.pallas_call(
        gather_kernel,
        out_shape=jax.ShapeDtypeStruct((64, 16, D), bf16),
        in_specs=[smem, anywhere],
        out_specs=anywhere,
        scratch_shapes=[pltpu.VMEM((64, 16, D), bf16), dma((4,)), dma((4,))],
        name="gather",
    )(source_rows, arrived)
    return (layer_out, kv_decode)


def solution(mesh):
    in_specs = (
        P(("dp", "tensor"), None, None),
        P(("dp", "tensor"), None, None),
        P(),
        P(),
        P(),
        P(None, None, "tensor"),
        P(),
        P(),
        P(),
        P(),
    )
    out_specs = (P(("dp", "tensor"), None, None), P("dp", "tensor", None))
    return jax.shard_map(local, mesh=mesh, in_specs=in_specs, out_specs=out_specs, check_vma=False)
```

```python
import functools

import jax
import jax.numpy as jnp
import numpy as np
from jax import lax
from jax.experimental import pallas as pl
from jax.experimental.pallas import tpu as pltpu
from jax.sharding import PartitionSpec as P

D = 1536
HEADS = 16
KV_HEADS = 8
HEAD_DIM = 96
NEW = 128
CTX = 512
KEYS = KV_HEADS * HEAD_DIM
RING = 4
CHIPS = RING * RING
MESH = pl.DeviceIdType.MESH

epsilon = 1e-05
rope_base = 100000.0
LANES = 384
TILE = 256
TILES = D // TILE
PARTS = 4
WIDE = D // PARTS


def messages():
    found = []

    def along(axis, shards, first):
        step = (1, 0) if axis == 0 else (0, 1)
        for shard in shards:
            for sign in (1, -1):
                found.append((shard, first, 2, (sign * step[0], sign * step[1]), "send"))
            for sign in (1, -1):
                source = (shard[0] - sign * step[0], shard[1] - sign * step[1])
                piece = first if sign == 1 else first + 1
                found.append((source, piece, 1, (sign * step[0], sign * step[1]), "pass"))

    along(0, [(0, 0)], 0)
    along(1, [(0, 0)], 2)
    along(1, [(0, 0)], 0)
    along(0, [(0, 0)], 2)
    along(1, [(-1, 0), (1, 0)], 0)
    along(0, [(0, -1), (0, 1)], 2)
    along(1, [(2, 0)], 0)
    along(0, [(0, 2)], 2)
    return found


MESSAGES = messages()
N_MSG = len(MESSAGES)


def wrapped(offset):
    return (offset[0] % RING, offset[1] % RING)


def arrival(message):
    shard, first, count, direction, _ = message
    return wrapped((shard[0] - direction[0], shard[1] - direction[1])), first, count


def stage_of(index):
    shard, first, count, _, _ = MESSAGES[index]
    if wrapped(shard) == (0, 0):
        return 0
    return 1 + max(stage_of(other) for other in sources(index))


def sources(index):
    shard, first, count, _, _ = MESSAGES[index]
    found = []
    for piece in range(first, first + count):
        for other, message in enumerate(MESSAGES):
            came, start, number = arrival(message)
            if came == wrapped(shard) and start <= piece < start + number:
                found.append(other)
    return sorted(set(found))


def norm_rows(values, gain):
    widened = values.astype(jnp.float32)
    factor = lax.rsqrt(jnp.mean(widened * widened, axis=-1, keepdims=True) + epsilon)
    return (widened * factor * gain).astype(jnp.bfloat16)


def dot(a, b):
    return lax.dot_general(a, b, (((1,), (0,)), ((), ())), preferred_element_type=jnp.float32)


def dot_nt(a, b):
    return lax.dot_general(a, b, (((1,), (1,)), ((), ())), preferred_element_type=jnp.float32)


def layer_kernel(
    order_ref,
    new_ref,
    prefix_ref,
    slots_ref,
    tokens_hbm,
    cached_hbm,
    gains_ref,
    rope_ref,
    w_qkv_hbm,
    w_out_hbm,
    own_hbm,
    layer_hbm,
    arrived_hbm,
    source_ref,
    by_slot,
    by_slot_rows,
    tokens,
    normed,
    w_qkv,
    w_out,
    context,
    weights,
    queries,
    fresh,
    attended,
    residual,
    posts,
    received_0,
    received_1,
    received_2,
    received_3,
    arranged,
    activated,
    kept,
    own_sum,
    to_partner,
    from_partner,
    to_pair,
    from_pair,
    local_sem,
    weight_send,
    weight_recv,
    kv_send,
    kv_recv,
    deal_send,
    deal_recv,
    post_send,
    post_recv,
    part_send,
    part_recv,
):
    z = lax.axis_index("dp")
    t = lax.axis_index("tensor")
    x, y, core = t // 8, lax.rem(t // 2, RING), lax.rem(t, 2)
    half = lax.rem(z, 2)
    pair_z = z + 1 - 2 * half
    partner = t + 1 - 2 * core
    member = half * 2 + core

    requests = [order_ref[(z * 32 + t) * 2 + j] for j in range(2)]
    new_counts = [new_ref[request] for request in requests]
    cached_counts = [prefix_ref[request] for request in requests]

    def tensor_at(dx, dy, other=0):
        there = lax.rem(core + other, 2)
        return (lax.rem(x + dx + RING, RING) * RING + lax.rem(y + dy + RING, RING)) * 2 + there

    def shard_at(offset):
        return lax.rem(x + offset[0] + RING, RING) * RING + lax.rem(y + offset[1] + RING, RING)

    loads = [
        pltpu.make_async_copy(
            own_hbm.at[:, pl.ds(half * 64, 64), :],
            weights.at[:, pl.ds(shard_at((0, 0)) * 64, 64), :],
            local_sem.at[0],
        ),
        pltpu.make_async_copy(tokens_hbm, tokens, local_sem.at[1]),
        pltpu.make_async_copy(w_qkv_hbm, w_qkv, local_sem.at[2]),
        pltpu.make_async_copy(cached_hbm, context, local_sem.at[3]),
        pltpu.make_async_copy(w_out_hbm, w_out, local_sem.at[4]),
    ]
    for load in loads:
        load.start()

    barrier = pltpu.get_barrier_semaphore()

    @pl.loop(1, 32)
    def _(step):
        pl.semaphore_signal(
            barrier, inc=1, device_id=(z, lax.rem(t + step, 32)), device_id_type=MESH
        )

    @pl.loop(1, 4)
    def _(step):
        pl.semaphore_signal(
            barrier, inc=1, device_id=(lax.rem(z + step, 4), t), device_id_type=MESH
        )

    pl.semaphore_wait(barrier, 34)

    def weight_copy(index):
        shard, first, count, direction, _ = MESSAGES[index]
        rows = pl.ds(pl.multiple_of(shard_at(wrapped(shard)) * 64 + 16 * first, 16), 16 * count)
        return pltpu.make_async_remote_copy(
            src_ref=weights.at[:, rows, :],
            dst_ref=weights.at[:, rows, :],
            send_sem=weight_send.at[index],
            recv_sem=weight_recv.at[index],
            device_id=(z, tensor_at(*direction)),
            device_id_type=MESH,
        )

    def weight_arrival(index):
        shard, first, count = arrival(MESSAGES[index])
        rows = pl.ds(pl.multiple_of(shard_at(shard) * 64 + 16 * first, 16), 16 * count)
        pltpu.make_async_remote_copy(
            src_ref=weights.at[:, rows, :],
            dst_ref=weights.at[:, rows, :],
            send_sem=weight_send.at[index],
            recv_sem=weight_recv.at[index],
            device_id=(z, partner),
            device_id_type=MESH,
        ).wait_recv()

    heard = set()

    def weight_stage(number):
        for index in range(N_MSG):
            if stage_of(index) == number:
                for other in sources(index) if number else []:
                    if other not in heard:
                        heard.add(other)
                        weight_arrival(other)
                weight_copy(index).start()

    def weight_ready(column):
        for index in range(N_MSG):
            if index not in heard and arrival(MESSAGES[index])[0][0] == column:
                heard.add(index)
                weight_arrival(index)

    loads[0].wait()
    weight_stage(0)

    loads[1].wait()
    for j in range(2):
        normed[pl.ds(j * NEW, NEW), :] = norm_rows(tokens[j], gains_ref[0:1, :])
    loads[2].wait()

    lane = lax.broadcasted_iota(jnp.int32, (NEW, LANES), 1)
    leading = lax.rem(lane, HEAD_DIM) < HEAD_DIM // 2

    def rotated(values, j):
        turn = cached_counts[j].astype(jnp.float32) * rope_ref[2, 0:8, :]
        turn_cosine, turn_sine = jnp.cos(turn)[0:1], jnp.sin(turn)[0:1]
        cosine = turn_cosine * rope_ref[0] - turn_sine * rope_ref[1]
        sine = turn_sine * rope_ref[0] + turn_cosine * rope_ref[1]
        sine = jnp.where(leading, -sine, sine)
        parts = []
        for n in range(values.shape[1] // LANES):
            part = values[:, n * LANES : (n + 1) * LANES]
            swapped = jnp.where(
                leading,
                pltpu.roll(part, LANES - HEAD_DIM // 2, 1),
                pltpu.roll(part, HEAD_DIM // 2, 1),
            )
            parts.append((part * cosine + swapped * sine).astype(jnp.bfloat16))
        return jnp.concatenate(parts, axis=1)

    def project(first):
        return dot(normed[...], w_qkv[:, first : first + KEYS])

    keys = project(D)
    for j in range(2):
        fresh[j, :, 0:KEYS] = rotated(keys[j * NEW : (j + 1) * NEW], j)
    values = project(D + KEYS)
    for j in range(2):
        fresh[j, :, KEYS:] = values[j * NEW : (j + 1) * NEW].astype(jnp.bfloat16)

    loads[3].wait()

    @pl.loop(0, 8)
    def _(step):
        j, block = step // 4, lax.rem(step, 4)
        new_count = new_ref[order_ref[(z * 32 + t) * 2 + j]]
        cached_count = prefix_ref[order_ref[(z * 32 + t) * 2 + j]]
        spot = block * 128 + lax.broadcasted_iota(jnp.int32, (128, NEW), 0)
        order = lax.broadcasted_iota(jnp.int32, (128, NEW), 1)
        chosen = (spot - cached_count == order) & (order < new_count)
        placed = dot(chosen.astype(jnp.bfloat16), fresh[j]).astype(jnp.bfloat16)
        rows = pl.ds(pl.multiple_of(block * 128, 128), 128)
        row = block * 128 + lax.broadcasted_iota(jnp.int32, (128, D), 0)
        context[j, rows, :] = jnp.where(row < cached_count, context[j, rows, :], placed)

    received = (received_0, received_1, received_2, received_3)

    def offset_at(step):
        turn, dx = step // 8, lax.rem(step // 2, RING)
        return dx, lax.rem(turn + dx, RING), lax.rem(step, 2)

    def kv_copy(part, step):
        target = tensor_at(*offset_at(step))
        columns = pl.ds(part * WIDE, WIDE)
        return pltpu.make_async_remote_copy(
            src_ref=context.at[:, pl.ds(pl.multiple_of(target * 16, 16), 16), columns],
            dst_ref=received[part].at[t],
            send_sem=kv_send.at[part, step],
            recv_sem=kv_recv.at[part, step],
            device_id=(z, target),
            device_id_type=MESH,
        )

    def kv_start(part):
        @pl.loop(1, 32)
        def _(step):
            kv_copy(part, step).start()

        for j in range(2):
            received[part][t, j] = context[
                j, pl.ds(pl.multiple_of(t * 16, 16), 16), part * WIDE : (part + 1) * WIDE
            ]

    for part in range(PARTS):
        kv_start(part)

    for n in range(2):
        some = project(n * KEYS)
        for j in range(2):
            queries[j, :, n * KEYS : (n + 1) * KEYS] = rotated(some[j * NEW : (j + 1) * NEW], j)

    weight_stage(1)

    along = lax.broadcasted_iota(jnp.int32, (64, 128), 1)
    across = lax.broadcasted_iota(jnp.int32, (64, 128), 0)
    spread = lax.broadcasted_iota(jnp.int32, (1, 128), 1)
    inside = along < 64

    def upright(row):
        return jnp.sum(jnp.where(along == across, row, 0), axis=1, keepdims=True)

    def add_slot(i, row):
        return jnp.where(spread == i, slots_ref[order_ref[z * 64 + i]], row)

    slots = lax.fori_loop(0, 64, add_slot, jnp.zeros((1, 128), jnp.int32))
    rank = jnp.sum(
        jnp.where((slots < upright(slots)) & inside, 1, 0), axis=1, keepdims=True
    )
    by_slot[...] = jnp.sum(jnp.where(rank == along, across, 0), axis=0, keepdims=True)

    def add_owner(i, row):
        return jnp.where(spread == slots_ref[order_ref[i]] - z * 64, i // 64, row)

    owners = lax.fori_loop(0, 256, add_owner, jnp.zeros((1, 128), jnp.int32))
    owner = upright(owners)
    earlier = jnp.sum(
        jnp.where((owner == owners) & (along < across), 1, 0), axis=1, keepdims=True
    )
    source = jnp.minimum(owner * 16 + earlier, 63)
    source_ref[...] = jnp.sum(jnp.where(along == across, source, 0), axis=0, keepdims=True)

    def attend(j):
        cached_count = cached_counts[j]
        spot = lax.broadcasted_iota(jnp.int32, (2 * NEW, CTX), 1)
        order = lax.rem(lax.broadcasted_iota(jnp.int32, (2 * NEW, CTX), 0), NEW)
        allowed = spot <= cached_count + order
        for h in range(KV_HEADS):
            at = h * 2 * HEAD_DIM
            both = jnp.concatenate(
                [queries[j, :, at : at + HEAD_DIM], queries[j, :, at + HEAD_DIM : at + 2 * HEAD_DIM]],
                axis=0,
            )
            key = context[j, :, h * HEAD_DIM : (h + 1) * HEAD_DIM]
            value = context[j, :, KEYS + h * HEAD_DIM : KEYS + (h + 1) * HEAD_DIM]
            scores = dot_nt(both, key) * HEAD_DIM ** (-0.5)
            scores = jnp.where(allowed, scores, -jnp.inf)
            exponent = jnp.exp(scores - jnp.max(scores, axis=-1, keepdims=True))
            total = jnp.sum(exponent, axis=-1, keepdims=True)
            mixed = (dot(exponent.astype(jnp.bfloat16), value) / total).astype(jnp.bfloat16)
            attended[j, :, at : at + 2 * HEAD_DIM] = jnp.concatenate(
                [mixed[:NEW], mixed[NEW:]], axis=1
            )

    def post_copy(kind, j):
        whose = member if kind < 2 else (1 - half) * 2 + core
        rows = posts.at[whose, pl.ds(j * NEW, NEW), :]
        return pltpu.make_async_remote_copy(
            src_ref=rows,
            dst_ref=rows,
            send_sem=post_send.at[kind, j],
            recv_sem=post_recv.at[kind, j],
            device_id=(pair_z, t) if kind == 1 else (z, partner),
            device_id_type=MESH,
        )

    def post_arrival(kind, j):
        whose = (half * 2 + 1 - core, (1 - half) * 2 + core, (1 - half) * 2 + 1 - core)[kind]
        rows = posts.at[whose, pl.ds(j * NEW, NEW), :]
        pltpu.make_async_remote_copy(
            src_ref=rows,
            dst_ref=rows,
            send_sem=post_send.at[kind, j],
            recv_sem=post_recv.at[kind, j],
            device_id=(z, partner),
            device_id_type=MESH,
        ).wait_recv()

    for j in range(2):
        attend(j)
        if j == 0:
            loads[4].wait()
        mixed = dot(attended[j], w_out[...])
        rounded = (tokens[j].astype(jnp.float32) + mixed).astype(jnp.bfloat16)
        residual[j] = rounded
        posts[member, pl.ds(j * NEW, NEW), :] = norm_rows(rounded, gains_ref[1:2, :])
        post_copy(1, j).start()
        post_copy(0, j).start()

    def deal_copy(part, step):
        target = lax.rem(z + step, 4)
        return pltpu.make_async_remote_copy(
            src_ref=arranged.at[part, pl.ds(pl.multiple_of(target * 16, 16), 16)],
            dst_ref=arrived_hbm.at[part, z],
            send_sem=deal_send.at[part, step],
            recv_sem=deal_recv.at[part, step],
            device_id=(target, t),
            device_id_type=MESH,
        )

    def own_deal(part):
        return pltpu.make_async_copy(
            arranged.at[part, pl.ds(pl.multiple_of(z * 16, 16), 16)],
            arrived_hbm.at[part, z],
            deal_send.at[part, 0],
        )

    def deal(part):
        @pl.loop(1, 32)
        def _(step):
            dx, dy, dc = offset_at(step)
            source = (
                lax.rem(x - dx + RING, RING) * RING + lax.rem(y - dy + RING, RING)
            ) * 2 + lax.rem(core + dc, 2)
            pltpu.make_async_remote_copy(
                src_ref=received[part].at[source],
                dst_ref=received[part].at[source],
                send_sem=kv_send.at[part, step],
                recv_sem=kv_recv.at[part, step],
                device_id=(z, partner),
                device_id_type=MESH,
            ).wait_recv()

        @pl.loop(0, 64)
        def _(row):
            slot = lax.rem(by_slot_rows[0, row], 64)
            arranged[part, row] = received[part][slot // 2, lax.rem(slot, 2)]

        for step in range(1, 4):
            deal_copy(part, step).start()
        own_deal(part).start()

    ordering = pltpu.make_async_copy(by_slot, by_slot_rows, local_sem.at[0])
    ordering.start()
    ordering.wait()
    deal(0)
    deal(1)
    post_arrival(1, 0)
    post_copy(2, 0).start()
    deal(2)
    post_arrival(1, 1)
    post_copy(2, 1).start()
    deal(3)

    def hidden(which, column):
        units = pl.ds(pl.multiple_of(lax.rem(x + column, RING) * TILE, TILE), TILE)

        @pl.loop(which * 2, which * 2 + 2)
        def _(m):
            rows = posts[m]
            gate = dot_nt(rows, weights[0, units, :])
            up = dot_nt(rows, weights[1, units, :])
            activated[m, :, units] = (gate / (1.0 + jnp.exp(-gate)) * up).astype(jnp.bfloat16)

    for j in range(2):
        post_arrival(0, j)
        post_arrival(2, j)
    weight_stage(2)
    weight_ready(0)
    hidden(1 - half, 0)
    hidden(half, 0)
    weight_stage(3)
    weight_ready(1)
    hidden(1 - half, 1)
    weight_ready(3)
    hidden(1 - half, 3)
    weight_ready(2)
    hidden(1 - half, 2)

    def part_copy(kind, n):
        here, there = ((to_partner.at[0, n], from_partner.at[0, n]), (to_pair.at[n], from_pair.at[n]), (to_partner.at[1, n], from_partner.at[1, n]))[kind]
        return pltpu.make_async_remote_copy(
            src_ref=here,
            dst_ref=there,
            send_sem=part_send.at[kind, n],
            recv_sem=part_recv.at[kind, n],
            device_id=(pair_z, t) if kind == 1 else (z, partner),
            device_id_type=MESH,
        )

    def down(which, core_at, n):
        columns = pl.ds(pl.multiple_of(n * TILE, TILE), TILE)
        return dot(activated[which * 2 + core_at], weights[2, :, columns])

    def add_up(n):
        part_copy(0, n).wait_recv()
        to_pair[n] = (kept[n] + from_partner[0, n].astype(jnp.float32)).astype(jnp.bfloat16)
        part_copy(1, n).start()

    @pl.loop(0, TILES)
    def _(n):
        to_partner[0, n] = down(1 - half, 1 - core, n).astype(jnp.bfloat16)
        part_copy(0, n).start()
        kept[n] = down(1 - half, core, n)

        @pl.when(n > 0)
        def _():
            add_up(n - 1)

    add_up(TILES - 1)

    for column in (1, 3, 2):
        hidden(half, column)

    @pl.loop(0, TILES)
    def _(n):
        to_partner[1, n] = down(half, 1 - core, n).astype(jnp.bfloat16)
        part_copy(2, n).start()
        own_sum[n] = down(half, core, n)

    for n in range(TILES):
        part_copy(2, n).wait_recv()
        part_copy(1, n).wait_recv()
        columns = slice(n * TILE, (n + 1) * TILE)
        for j in range(2):
            rows = slice(j * NEW, (j + 1) * NEW)
            row = lax.broadcasted_iota(jnp.int32, (NEW, TILE), 0)
            total = (
                residual[j, :, columns].astype(jnp.float32)
                + own_sum[n, rows]
                + from_partner[1, n, rows].astype(jnp.float32)
                + from_pair[n, rows].astype(jnp.float32)
            )
            tokens[j, :, columns] = jnp.where(row < new_counts[j], total, 0.0).astype(jnp.bfloat16)
    store = pltpu.make_async_copy(tokens, layer_hbm, local_sem.at[1])
    store.start()

    for part in range(PARTS):
        for step in range(1, 4):
            source = lax.rem(z - step + 4, 4)
            pltpu.make_async_remote_copy(
                src_ref=arranged.at[part, pl.ds(0, 16)],
                dst_ref=arrived_hbm.at[part, source],
                send_sem=deal_send.at[part, step],
                recv_sem=deal_recv.at[part, step],
                device_id=(source, t),
                device_id_type=MESH,
            ).wait_recv()
            deal_copy(part, step).wait_send()
        own_deal(part).wait()

        @pl.loop(1, 32)
        def _(step):
            kv_copy(part, step).wait_send()

    for index in range(N_MSG):
        weight_copy(index).wait_send()
    for kind in range(3):
        for j in range(2):
            post_copy(kind, j).wait_send()
        for n in range(TILES):
            part_copy(kind, n).wait_send()
    store.wait()


def gather_kernel(index_ref, arrived_hbm, out_hbm, rows, load_sem, store_sem):
    def load(s, part):
        source = index_ref[0, s]
        return pltpu.make_async_copy(
            arrived_hbm.at[part, source // 16, lax.rem(source, 16)],
            rows.at[s, :, pl.ds(part * WIDE, WIDE)],
            load_sem.at[s // 16],
        )

    def store(block):
        span = pl.ds(pl.multiple_of(block * 16, 16), 16)
        return pltpu.make_async_copy(rows.at[span], out_hbm.at[span], store_sem.at[block])

    @pl.loop(0, 64)
    def _(s):
        for part in range(PARTS):
            load(s, part).start()

    @pl.loop(0, 4)
    def _(block):
        span = pl.ds(pl.multiple_of(block * 16, 16), 16)
        pltpu.make_async_copy(rows.at[span], rows.at[span], load_sem.at[block]).wait()
        store(block).start()

    @pl.loop(0, 4)
    def _(block):
        store(block).wait()


def frequencies():
    lane = np.arange(LANES) % HEAD_DIM
    return rope_base ** (-2.0 * (lane % (HEAD_DIM // 2)) / HEAD_DIM)


def local(
    tokens,
    cached,
    norm_gains,
    w_qkv,
    w_out,
    mlp_weights,
    request_order,
    new_lengths,
    cached_lengths,
    decode_slots,
):
    frequency = frequencies()
    angle = np.arange(NEW)[:, None] * frequency[None, :]
    tables = [np.cos(angle), np.sin(angle), np.broadcast_to(frequency, angle.shape)]
    rope = jnp.asarray(np.stack(tables), jnp.float32)
    own = jnp.transpose(mlp_weights, (0, 2, 1))

    bf16 = jnp.bfloat16
    smem = pl.BlockSpec(memory_space=pltpu.SMEM)
    vmem = pl.BlockSpec(memory_space=pltpu.VMEM)
    anywhere = pl.BlockSpec(memory_space=pl.ANY)
    dma = pltpu.SemaphoreType.DMA
    layer_out, arrived, source_rows = pl.pallas_call(
        layer_kernel,
        out_shape=(
            jax.ShapeDtypeStruct((2, NEW, D), bf16),
            jax.ShapeDtypeStruct((PARTS, 4, 16, 16, WIDE), bf16),
            jax.ShapeDtypeStruct((1, 128), jnp.int32),
        ),
        in_specs=[smem] * 4 + [anywhere, anywhere, vmem, vmem, anywhere, anywhere, anywhere],
        out_specs=(anywhere, anywhere, vmem),
        scratch_shapes=[
            pltpu.VMEM((1, 128), jnp.int32),
            pltpu.SMEM((1, 128), jnp.int32),
            pltpu.VMEM((2, NEW, D), bf16),
            pltpu.VMEM((2 * NEW, D), bf16),
            pltpu.VMEM((D, 2 * D), bf16),
            pltpu.VMEM((D, D), bf16),
            pltpu.VMEM((2, CTX, D), bf16),
            pltpu.VMEM((3, 1024, D), bf16),
            pltpu.VMEM((2, NEW, D), bf16),
            pltpu.VMEM((2, NEW, D), bf16),
            pltpu.VMEM((2, NEW, D), bf16),
            pltpu.VMEM((2, NEW, D), bf16),
            pltpu.VMEM((4, 2 * NEW, D), bf16),
            *[pltpu.VMEM((32, 2, 16, WIDE), bf16) for _ in range(PARTS)],
            pltpu.VMEM((PARTS, 64, 16, WIDE), bf16),
            pltpu.VMEM((4, 2 * NEW, 1024), bf16),
            pltpu.VMEM((TILES, 2 * NEW, TILE), jnp.float32),
            pltpu.VMEM((TILES, 2 * NEW, TILE), jnp.float32),
            pltpu.VMEM((2, TILES, 2 * NEW, TILE), bf16),
            pltpu.VMEM((2, TILES, 2 * NEW, TILE), bf16),
            pltpu.VMEM((TILES, 2 * NEW, TILE), bf16),
            pltpu.VMEM((TILES, 2 * NEW, TILE), bf16),
            dma((5,)),
            dma((N_MSG,)),
            dma((N_MSG,)),
            dma((PARTS, 32)),
            dma((PARTS, 32)),
            dma((PARTS, 4)),
            dma((PARTS, 4)),
            dma((3, 2)),
            dma((3, 2)),
            dma((3, TILES)),
            dma((3, TILES)),
        ],
        compiler_params=pltpu.CompilerParams(
            collective_id=0, has_side_effects=True, vmem_limit_bytes=67_000_000
        ),
        name="layer",
    )(
        request_order,
        new_lengths,
        cached_lengths,
        decode_slots,
        tokens,
        cached,
        norm_gains,
        rope,
        w_qkv,
        w_out,
        own,
    )

    kv_decode = pl.pallas_call(
        gather_kernel,
        out_shape=jax.ShapeDtypeStruct((64, 16, D), bf16),
        in_specs=[smem, anywhere],
        out_specs=anywhere,
        scratch_shapes=[pltpu.VMEM((64, 16, D), bf16), dma((4,)), dma((4,))],
        name="gather",
    )(source_rows, arrived)
    return (layer_out, kv_decode)


def solution(mesh):
    in_specs = (
        P(("dp", "tensor"), None, None),
        P(("dp", "tensor"), None, None),
        P(),
        P(),
        P(),
        P(None, None, "tensor"),
        P(),
        P(),
        P(),
        P(),
    )
    out_specs = (P(("dp", "tensor"), None, None), P("dp", "tensor", None))
    return jax.shard_map(local, mesh=mesh, in_specs=in_specs, out_specs=out_specs, check_vma=False)
```

```python
import functools

import jax
import jax.numpy as jnp
import numpy as np
from jax import lax
from jax.experimental import pallas as pl
from jax.experimental.pallas import tpu as pltpu
from jax.sharding import PartitionSpec as P

D = 1536
HEADS = 16
KV_HEADS = 8
HEAD_DIM = 96
NEW = 128
CTX = 512
KEYS = KV_HEADS * HEAD_DIM
RING = 4
CHIPS = RING * RING
MESH = pl.DeviceIdType.MESH

epsilon = 1e-05
rope_base = 100000.0
LANES = 384
TILE = 256
TILES = D // TILE
PARTS = 4
WIDE = D // PARTS


def messages():
    found = []

    def along(axis, shards, first):
        step = (1, 0) if axis == 0 else (0, 1)
        for shard in shards:
            for sign in (1, -1):
                found.append((shard, first, 2, (sign * step[0], sign * step[1]), "send"))
            for sign in (1, -1):
                source = (shard[0] - sign * step[0], shard[1] - sign * step[1])
                piece = first if sign == 1 else first + 1
                found.append((source, piece, 1, (sign * step[0], sign * step[1]), "pass"))

    along(0, [(0, 0)], 0)
    along(1, [(0, 0)], 2)
    along(1, [(0, 0)], 0)
    along(0, [(0, 0)], 2)
    along(1, [(-1, 0), (1, 0)], 0)
    along(0, [(0, -1), (0, 1)], 2)
    along(1, [(2, 0)], 0)
    along(0, [(0, 2)], 2)
    return found


MESSAGES = messages()
N_MSG = len(MESSAGES)


def wrapped(offset):
    return (offset[0] % RING, offset[1] % RING)


def arrival(message):
    shard, first, count, direction, _ = message
    return wrapped((shard[0] - direction[0], shard[1] - direction[1])), first, count


def stage_of(index):
    shard, first, count, _, _ = MESSAGES[index]
    if wrapped(shard) == (0, 0):
        return 0
    return 1 + max(stage_of(other) for other in sources(index))


def sources(index):
    shard, first, count, _, _ = MESSAGES[index]
    found = []
    for piece in range(first, first + count):
        for other, message in enumerate(MESSAGES):
            came, start, number = arrival(message)
            if came == wrapped(shard) and start <= piece < start + number:
                found.append(other)
    return sorted(set(found))


def norm_rows(values, gain):
    widened = values.astype(jnp.float32)
    factor = lax.rsqrt(jnp.mean(widened * widened, axis=-1, keepdims=True) + epsilon)
    return (widened * factor * gain).astype(jnp.bfloat16)


def dot(a, b):
    return lax.dot_general(a, b, (((1,), (0,)), ((), ())), preferred_element_type=jnp.float32)


def dot_nt(a, b):
    return lax.dot_general(a, b, (((1,), (1,)), ((), ())), preferred_element_type=jnp.float32)


def layer_kernel(
    order_ref,
    new_ref,
    prefix_ref,
    slots_ref,
    tokens_hbm,
    cached_hbm,
    gains_ref,
    rope_ref,
    w_qkv_hbm,
    w_out_hbm,
    own_hbm,
    layer_hbm,
    arrived_hbm,
    source_ref,
    by_slot,
    by_slot_rows,
    tokens,
    normed,
    w_qkv,
    w_out,
    context,
    weights,
    queries,
    fresh,
    attended,
    residual,
    posts,
    received_0,
    received_1,
    received_2,
    received_3,
    arranged,
    activated,
    kept,
    own_sum,
    to_partner,
    from_partner,
    to_pair,
    from_pair,
    local_sem,
    store_sem,
    weight_send,
    weight_recv,
    kv_send,
    kv_recv,
    deal_send,
    deal_recv,
    post_send,
    post_recv,
    part_send,
    part_recv,
):
    z = lax.axis_index("dp")
    t = lax.axis_index("tensor")
    x, y, core = t // 8, lax.rem(t // 2, RING), lax.rem(t, 2)
    half = lax.rem(z, 2)
    pair_z = z + 1 - 2 * half
    partner = t + 1 - 2 * core
    member = half * 2 + core

    requests = [order_ref[(z * 32 + t) * 2 + j] for j in range(2)]
    new_counts = [new_ref[request] for request in requests]
    cached_counts = [prefix_ref[request] for request in requests]

    def tensor_at(dx, dy, other=0):
        there = lax.rem(core + other, 2)
        return (lax.rem(x + dx + RING, RING) * RING + lax.rem(y + dy + RING, RING)) * 2 + there

    def shard_at(offset):
        return lax.rem(x + offset[0] + RING, RING) * RING + lax.rem(y + offset[1] + RING, RING)

    loads = [
        pltpu.make_async_copy(
            own_hbm.at[:, pl.ds(half * 64, 64), :],
            weights.at[:, pl.ds(shard_at((0, 0)) * 64, 64), :],
            local_sem.at[0],
        ),
        pltpu.make_async_copy(tokens_hbm, tokens, local_sem.at[1]),
        pltpu.make_async_copy(w_qkv_hbm, w_qkv, local_sem.at[2]),
        pltpu.make_async_copy(cached_hbm, context, local_sem.at[3]),
        pltpu.make_async_copy(w_out_hbm, w_out, local_sem.at[4]),
    ]
    for load in loads:
        load.start()

    barrier = pltpu.get_barrier_semaphore()

    @pl.loop(1, 32)
    def _(step):
        pl.semaphore_signal(
            barrier, inc=1, device_id=(z, lax.rem(t + step, 32)), device_id_type=MESH
        )

    @pl.loop(1, 4)
    def _(step):
        pl.semaphore_signal(
            barrier, inc=1, device_id=(lax.rem(z + step, 4), t), device_id_type=MESH
        )

    pl.semaphore_wait(barrier, 34)

    def weight_copy(index):
        shard, first, count, direction, _ = MESSAGES[index]
        rows = pl.ds(pl.multiple_of(shard_at(wrapped(shard)) * 64 + 16 * first, 16), 16 * count)
        return pltpu.make_async_remote_copy(
            src_ref=weights.at[:, rows, :],
            dst_ref=weights.at[:, rows, :],
            send_sem=weight_send.at[index],
            recv_sem=weight_recv.at[index],
            device_id=(z, tensor_at(*direction)),
            device_id_type=MESH,
        )

    def weight_arrival(index):
        shard, first, count = arrival(MESSAGES[index])
        rows = pl.ds(pl.multiple_of(shard_at(shard) * 64 + 16 * first, 16), 16 * count)
        pltpu.make_async_remote_copy(
            src_ref=weights.at[:, rows, :],
            dst_ref=weights.at[:, rows, :],
            send_sem=weight_send.at[index],
            recv_sem=weight_recv.at[index],
            device_id=(z, partner),
            device_id_type=MESH,
        ).wait_recv()

    heard = set()

    def weight_stage(number, kinds=("send", "pass")):
        for index in range(N_MSG):
            if stage_of(index) == number and MESSAGES[index][4] in kinds:
                for other in sources(index) if number else []:
                    if other not in heard:
                        heard.add(other)
                        weight_arrival(other)
                weight_copy(index).start()

    def weight_ready(column):
        for index in range(N_MSG):
            if index not in heard and arrival(MESSAGES[index])[0][0] == column:
                heard.add(index)
                weight_arrival(index)

    loads[0].wait()
    weight_stage(0)

    loads[1].wait()
    for j in range(2):
        normed[pl.ds(j * NEW, NEW), :] = norm_rows(tokens[j], gains_ref[0:1, :])
    loads[2].wait()

    lane = lax.broadcasted_iota(jnp.int32, (NEW, LANES), 1)
    leading = lax.rem(lane, HEAD_DIM) < HEAD_DIM // 2

    def rotated(values, j):
        turn = cached_counts[j].astype(jnp.float32) * rope_ref[2, 0:8, :]
        turn_cosine, turn_sine = jnp.cos(turn)[0:1], jnp.sin(turn)[0:1]
        cosine = turn_cosine * rope_ref[0] - turn_sine * rope_ref[1]
        sine = turn_sine * rope_ref[0] + turn_cosine * rope_ref[1]
        sine = jnp.where(leading, -sine, sine)
        parts = []
        for n in range(values.shape[1] // LANES):
            part = values[:, n * LANES : (n + 1) * LANES]
            swapped = jnp.where(
                leading,
                pltpu.roll(part, LANES - HEAD_DIM // 2, 1),
                pltpu.roll(part, HEAD_DIM // 2, 1),
            )
            parts.append((part * cosine + swapped * sine).astype(jnp.bfloat16))
        return jnp.concatenate(parts, axis=1)

    def project(first):
        return dot(normed[...], w_qkv[:, first : first + KEYS])

    keys = project(D)
    for j in range(2):
        fresh[j, :, 0:KEYS] = rotated(keys[j * NEW : (j + 1) * NEW], j)
    values = project(D + KEYS)
    for j in range(2):
        fresh[j, :, KEYS:] = values[j * NEW : (j + 1) * NEW].astype(jnp.bfloat16)

    loads[3].wait()

    @pl.loop(0, 8)
    def _(step):
        j, block = step // 4, lax.rem(step, 4)
        new_count = new_ref[order_ref[(z * 32 + t) * 2 + j]]
        cached_count = prefix_ref[order_ref[(z * 32 + t) * 2 + j]]
        spot = block * 128 + lax.broadcasted_iota(jnp.int32, (128, NEW), 0)
        order = lax.broadcasted_iota(jnp.int32, (128, NEW), 1)
        chosen = (spot - cached_count == order) & (order < new_count)
        placed = dot(chosen.astype(jnp.bfloat16), fresh[j]).astype(jnp.bfloat16)
        rows = pl.ds(pl.multiple_of(block * 128, 128), 128)
        row = block * 128 + lax.broadcasted_iota(jnp.int32, (128, D), 0)
        context[j, rows, :] = jnp.where(row < cached_count, context[j, rows, :], placed)

    received = (received_0, received_1, received_2, received_3)

    def offset_at(step):
        turn, dx = step // 8, lax.rem(step // 2, RING)
        return dx, lax.rem(turn + dx, RING), lax.rem(step, 2)

    def kv_copy(part, step):
        target = tensor_at(*offset_at(step))
        columns = pl.ds(part * WIDE, WIDE)
        return pltpu.make_async_remote_copy(
            src_ref=context.at[:, pl.ds(pl.multiple_of(target * 16, 16), 16), columns],
            dst_ref=received[part].at[t],
            send_sem=kv_send.at[part, step],
            recv_sem=kv_recv.at[part, step],
            device_id=(z, target),
            device_id_type=MESH,
        )

    def kv_start(part):
        @pl.loop(1, 32)
        def _(step):
            kv_copy(part, step).start()

        for j in range(2):
            received[part][t, j] = context[
                j, pl.ds(pl.multiple_of(t * 16, 16), 16), part * WIDE : (part + 1) * WIDE
            ]

    kv_start(0)

    for n in range(2):
        some = project(n * KEYS)
        for j in range(2):
            queries[j, :, n * KEYS : (n + 1) * KEYS] = rotated(some[j * NEW : (j + 1) * NEW], j)

    weight_stage(1)
    for part in range(1, PARTS):
        kv_start(part)

    along = lax.broadcasted_iota(jnp.int32, (64, 128), 1)
    across = lax.broadcasted_iota(jnp.int32, (64, 128), 0)
    spread = lax.broadcasted_iota(jnp.int32, (1, 128), 1)
    inside = along < 64

    def upright(row):
        return jnp.sum(jnp.where(along == across, row, 0), axis=1, keepdims=True)

    def add_slot(i, row):
        return jnp.where(spread == i, slots_ref[order_ref[z * 64 + i]], row)

    slots = lax.fori_loop(0, 64, add_slot, jnp.zeros((1, 128), jnp.int32))
    rank = jnp.sum(
        jnp.where((slots < upright(slots)) & inside, 1, 0), axis=1, keepdims=True
    )
    by_slot[...] = jnp.sum(jnp.where(rank == along, across, 0), axis=0, keepdims=True)

    def add_owner(i, row):
        return jnp.where(spread == slots_ref[order_ref[i]] - z * 64, i // 64, row)

    owners = lax.fori_loop(0, 256, add_owner, jnp.zeros((1, 128), jnp.int32))
    owner = upright(owners)
    earlier = jnp.sum(
        jnp.where((owner == owners) & (along < across), 1, 0), axis=1, keepdims=True
    )
    source = jnp.minimum(owner * 16 + earlier, 63)
    source_ref[...] = jnp.sum(jnp.where(along == across, source, 0), axis=0, keepdims=True)

    def attend(j):
        cached_count = cached_counts[j]
        spot = lax.broadcasted_iota(jnp.int32, (2 * NEW, CTX), 1)
        order = lax.rem(lax.broadcasted_iota(jnp.int32, (2 * NEW, CTX), 0), NEW)
        allowed = spot <= cached_count + order
        for h in range(KV_HEADS):
            at = h * 2 * HEAD_DIM
            both = jnp.concatenate(
                [queries[j, :, at : at + HEAD_DIM], queries[j, :, at + HEAD_DIM : at + 2 * HEAD_DIM]],
                axis=0,
            )
            key = context[j, :, h * HEAD_DIM : (h + 1) * HEAD_DIM]
            value = context[j, :, KEYS + h * HEAD_DIM : KEYS + (h + 1) * HEAD_DIM]
            scores = dot_nt(both, key) * HEAD_DIM ** (-0.5)
            scores = jnp.where(allowed, scores, -jnp.inf)
            exponent = jnp.exp(scores - jnp.max(scores, axis=-1, keepdims=True))
            total = jnp.sum(exponent, axis=-1, keepdims=True)
            mixed = (dot(exponent.astype(jnp.bfloat16), value) / total).astype(jnp.bfloat16)
            attended[j, :, at : at + 2 * HEAD_DIM] = jnp.concatenate(
                [mixed[:NEW], mixed[NEW:]], axis=1
            )

    def post_copy(kind, j):
        whose = member if kind < 2 else (1 - half) * 2 + core
        rows = posts.at[whose, pl.ds(j * NEW, NEW), :]
        return pltpu.make_async_remote_copy(
            src_ref=rows,
            dst_ref=rows,
            send_sem=post_send.at[kind, j],
            recv_sem=post_recv.at[kind, j],
            device_id=(pair_z, t) if kind == 1 else (z, partner),
            device_id_type=MESH,
        )

    def post_arrival(kind, j):
        whose = (half * 2 + 1 - core, (1 - half) * 2 + core, (1 - half) * 2 + 1 - core)[kind]
        rows = posts.at[whose, pl.ds(j * NEW, NEW), :]
        pltpu.make_async_remote_copy(
            src_ref=rows,
            dst_ref=rows,
            send_sem=post_send.at[kind, j],
            recv_sem=post_recv.at[kind, j],
            device_id=(z, partner),
            device_id_type=MESH,
        ).wait_recv()

    for j in range(2):
        attend(j)
        if j == 0:
            loads[4].wait()
        mixed = dot(attended[j], w_out[...])
        rounded = (tokens[j].astype(jnp.float32) + mixed).astype(jnp.bfloat16)
        residual[j] = rounded
        posts[member, pl.ds(j * NEW, NEW), :] = norm_rows(rounded, gains_ref[1:2, :])
        post_copy(1, j).start()
        post_copy(0, j).start()

    def deal_copy(part, step):
        target = lax.rem(z + step, 4)
        return pltpu.make_async_remote_copy(
            src_ref=arranged.at[part, pl.ds(pl.multiple_of(target * 16, 16), 16)],
            dst_ref=arrived_hbm.at[part, z],
            send_sem=deal_send.at[part, step],
            recv_sem=deal_recv.at[part, step],
            device_id=(target, t),
            device_id_type=MESH,
        )

    def own_deal(part):
        return pltpu.make_async_copy(
            arranged.at[part, pl.ds(pl.multiple_of(z * 16, 16), 16)],
            arrived_hbm.at[part, z],
            deal_send.at[part, 0],
        )

    def deal(part):
        @pl.loop(1, 32)
        def _(step):
            dx, dy, dc = offset_at(step)
            source = (
                lax.rem(x - dx + RING, RING) * RING + lax.rem(y - dy + RING, RING)
            ) * 2 + lax.rem(core + dc, 2)
            pltpu.make_async_remote_copy(
                src_ref=received[part].at[source],
                dst_ref=received[part].at[source],
                send_sem=kv_send.at[part, step],
                recv_sem=kv_recv.at[part, step],
                device_id=(z, partner),
                device_id_type=MESH,
            ).wait_recv()

        @pl.loop(0, 64)
        def _(row):
            slot = lax.rem(by_slot_rows[0, row], 64)
            arranged[part, row] = received[part][slot // 2, lax.rem(slot, 2)]

        for step in range(1, 4):
            deal_copy(part, step).start()
        own_deal(part).start()

    ordering = pltpu.make_async_copy(by_slot, by_slot_rows, local_sem.at[0])
    ordering.start()
    ordering.wait()
    deal(0)
    for j in range(2):
        post_arrival(1, j)
        post_copy(2, j).start()
    weight_stage(2, ("send",))
    weight_stage(2, ("pass",))
    deal(1)
    deal(2)

    def hidden(which, column):
        units = pl.ds(pl.multiple_of(lax.rem(x + column, RING) * TILE, TILE), TILE)

        @pl.loop(which * 2, which * 2 + 2)
        def _(m):
            rows = posts[m]
            gate = dot_nt(rows, weights[0, units, :])
            up = dot_nt(rows, weights[1, units, :])
            activated[m, :, units] = (gate / (1.0 + jnp.exp(-gate)) * up).astype(jnp.bfloat16)

    for j in range(2):
        post_arrival(0, j)
        post_arrival(2, j)
    weight_ready(0)
    hidden(1 - half, 0)
    deal(3)
    hidden(half, 0)
    weight_stage(3)
    weight_ready(1)
    hidden(1 - half, 1)
    weight_ready(3)
    hidden(1 - half, 3)
    weight_ready(2)
    hidden(1 - half, 2)

    def part_copy(kind, n):
        here, there = ((to_partner.at[0, n], from_partner.at[0, n]), (to_pair.at[n], from_pair.at[n]), (to_partner.at[1, n], from_partner.at[1, n]))[kind]
        return pltpu.make_async_remote_copy(
            src_ref=here,
            dst_ref=there,
            send_sem=part_send.at[kind, n],
            recv_sem=part_recv.at[kind, n],
            device_id=(pair_z, t) if kind == 1 else (z, partner),
            device_id_type=MESH,
        )

    def down(which, core_at, n):
        columns = pl.ds(pl.multiple_of(n * TILE, TILE), TILE)
        return dot(activated[which * 2 + core_at], weights[2, :, columns])

    def add_up(n):
        part_copy(0, n).wait_recv()
        to_pair[n] = (kept[n] + from_partner[0, n].astype(jnp.float32)).astype(jnp.bfloat16)
        part_copy(1, n).start()

    @pl.loop(0, TILES)
    def _(n):
        to_partner[0, n] = down(1 - half, 1 - core, n).astype(jnp.bfloat16)
        part_copy(0, n).start()
        kept[n] = down(1 - half, core, n)

        @pl.when(n > 0)
        def _():
            add_up(n - 1)

    add_up(TILES - 1)

    for column in (1, 3, 2):
        hidden(half, column)

    @pl.loop(0, TILES)
    def _(n):
        to_partner[1, n] = down(half, 1 - core, n).astype(jnp.bfloat16)
        part_copy(2, n).start()
        own_sum[n] = down(half, core, n)

    def store(n):
        columns = pl.ds(n * TILE, TILE)
        return pltpu.make_async_copy(
            tokens.at[:, :, columns], layer_hbm.at[:, :, columns], store_sem.at[n]
        )

    for n in range(TILES):
        part_copy(2, n).wait_recv()
        part_copy(1, n).wait_recv()
        columns = slice(n * TILE, (n + 1) * TILE)
        for j in range(2):
            rows = slice(j * NEW, (j + 1) * NEW)
            row = lax.broadcasted_iota(jnp.int32, (NEW, TILE), 0)
            total = (
                residual[j, :, columns].astype(jnp.float32)
                + own_sum[n, rows]
                + from_partner[1, n, rows].astype(jnp.float32)
                + from_pair[n, rows].astype(jnp.float32)
            )
            tokens[j, :, columns] = jnp.where(row < new_counts[j], total, 0.0).astype(jnp.bfloat16)
        store(n).start()

    for part in range(PARTS):
        for step in range(1, 4):
            source = lax.rem(z - step + 4, 4)
            pltpu.make_async_remote_copy(
                src_ref=arranged.at[part, pl.ds(0, 16)],
                dst_ref=arrived_hbm.at[part, source],
                send_sem=deal_send.at[part, step],
                recv_sem=deal_recv.at[part, step],
                device_id=(source, t),
                device_id_type=MESH,
            ).wait_recv()
            deal_copy(part, step).wait_send()
        own_deal(part).wait()

        @pl.loop(1, 32)
        def _(step):
            kv_copy(part, step).wait_send()

    for index in range(N_MSG):
        weight_copy(index).wait_send()
    for kind in range(3):
        for j in range(2):
            post_copy(kind, j).wait_send()
        for n in range(TILES):
            part_copy(kind, n).wait_send()
    for n in range(TILES):
        store(n).wait()


def gather_kernel(index_ref, arrived_hbm, out_hbm, rows, load_sem, store_sem):
    def span_at(block):
        return pl.ds(pl.multiple_of(block * 16, 16), 16)

    def store(block, part):
        span = span_at(block)
        return pltpu.make_async_copy(
            rows.at[span, part],
            out_hbm.at[span, :, pl.ds(part * WIDE, WIDE)],
            store_sem.at[block, part],
        )

    @pl.loop(0, 64)
    def _(s):
        source = index_ref[0, s]
        pltpu.make_async_copy(
            arrived_hbm.at[:, source // 16, lax.rem(source, 16)],
            rows.at[s],
            load_sem.at[s // 16],
        ).start()

    for block in range(4):
        span = span_at(block)
        pltpu.make_async_copy(rows.at[span], rows.at[span], load_sem.at[block]).wait()
        for part in range(PARTS):
            store(block, part).start()
    for block in range(4):
        for part in range(PARTS):
            store(block, part).wait()


def frequencies():
    lane = np.arange(LANES) % HEAD_DIM
    return rope_base ** (-2.0 * (lane % (HEAD_DIM // 2)) / HEAD_DIM)


def local(
    tokens,
    cached,
    norm_gains,
    w_qkv,
    w_out,
    mlp_weights,
    request_order,
    new_lengths,
    cached_lengths,
    decode_slots,
):
    frequency = frequencies()
    angle = np.arange(NEW)[:, None] * frequency[None, :]
    tables = [np.cos(angle), np.sin(angle), np.broadcast_to(frequency, angle.shape)]
    rope = jnp.asarray(np.stack(tables), jnp.float32)
    own = jnp.transpose(mlp_weights, (0, 2, 1))

    bf16 = jnp.bfloat16
    smem = pl.BlockSpec(memory_space=pltpu.SMEM)
    vmem = pl.BlockSpec(memory_space=pltpu.VMEM)
    anywhere = pl.BlockSpec(memory_space=pl.ANY)
    dma = pltpu.SemaphoreType.DMA
    layer_out, arrived, source_rows = pl.pallas_call(
        layer_kernel,
        out_shape=(
            jax.ShapeDtypeStruct((2, NEW, D), bf16),
            jax.ShapeDtypeStruct((PARTS, 4, 16, 16, WIDE), bf16),
            jax.ShapeDtypeStruct((1, 128), jnp.int32),
        ),
        in_specs=[smem] * 4 + [anywhere, anywhere, vmem, vmem, anywhere, anywhere, anywhere],
        out_specs=(anywhere, anywhere, vmem),
        scratch_shapes=[
            pltpu.VMEM((1, 128), jnp.int32),
            pltpu.SMEM((1, 128), jnp.int32),
            pltpu.VMEM((2, NEW, D), bf16),
            pltpu.VMEM((2 * NEW, D), bf16),
            pltpu.VMEM((D, 2 * D), bf16),
            pltpu.VMEM((D, D), bf16),
            pltpu.VMEM((2, CTX, D), bf16),
            pltpu.VMEM((3, 1024, D), bf16),
            pltpu.VMEM((2, NEW, D), bf16),
            pltpu.VMEM((2, NEW, D), bf16),
            pltpu.VMEM((2, NEW, D), bf16),
            pltpu.VMEM((2, NEW, D), bf16),
            pltpu.VMEM((4, 2 * NEW, D), bf16),
            *[pltpu.VMEM((32, 2, 16, WIDE), bf16) for _ in range(PARTS)],
            pltpu.VMEM((PARTS, 64, 16, WIDE), bf16),
            pltpu.VMEM((4, 2 * NEW, 1024), bf16),
            pltpu.VMEM((TILES, 2 * NEW, TILE), jnp.float32),
            pltpu.VMEM((TILES, 2 * NEW, TILE), jnp.float32),
            pltpu.VMEM((2, TILES, 2 * NEW, TILE), bf16),
            pltpu.VMEM((2, TILES, 2 * NEW, TILE), bf16),
            pltpu.VMEM((TILES, 2 * NEW, TILE), bf16),
            pltpu.VMEM((TILES, 2 * NEW, TILE), bf16),
            dma((5,)),
            dma((TILES,)),
            dma((N_MSG,)),
            dma((N_MSG,)),
            dma((PARTS, 32)),
            dma((PARTS, 32)),
            dma((PARTS, 4)),
            dma((PARTS, 4)),
            dma((3, 2)),
            dma((3, 2)),
            dma((3, TILES)),
            dma((3, TILES)),
        ],
        compiler_params=pltpu.CompilerParams(
            collective_id=0, has_side_effects=True, vmem_limit_bytes=67_000_000
        ),
        name="layer",
    )(
        request_order,
        new_lengths,
        cached_lengths,
        decode_slots,
        tokens,
        cached,
        norm_gains,
        rope,
        w_qkv,
        w_out,
        own,
    )

    kv_decode = pl.pallas_call(
        gather_kernel,
        out_shape=jax.ShapeDtypeStruct((64, 16, D), bf16),
        in_specs=[smem, anywhere],
        out_specs=anywhere,
        scratch_shapes=[pltpu.VMEM((64, PARTS, 16, WIDE), bf16), dma((4,)), dma((4, PARTS))],
        name="gather",
    )(source_rows, arrived)
    return (layer_out, kv_decode)


def solution(mesh):
    in_specs = (
        P(("dp", "tensor"), None, None),
        P(("dp", "tensor"), None, None),
        P(),
        P(),
        P(),
        P(None, None, "tensor"),
        P(),
        P(),
        P(),
        P(),
    )
    out_specs = (P(("dp", "tensor"), None, None), P("dp", "tensor", None))
    return jax.shard_map(local, mesh=mesh, in_specs=in_specs, out_specs=out_specs, check_vma=False)
```
